32 devices in a mesh: pt: 8 (over y, x, core), md: 4 (over z).
Axes of the slice: x: 2, y: 2, z: 4, core: 2. Of those that a mesh axis runs over, the one named last changes fastest.
Arguments:
- grid_index: int32 [3, 8192], P(None, 'pt'), may hold values from 0 to 255, as said below
- wavenumbers: int32 [3, 32768], P(None, 'md'), may hold values from -16 to 15, as said below
- test_block: int32 [32768, 256], P('md'), may hold values from -64 to 63
- slab_counts: int32 [8], P('pt'), may hold values from 1 to 1024, as said below
Outputs:
- adjoint_sketch: float32 [32768, 512], P(('md', 'pt'))
The draws below stay inside these ranges and needn't reach their ends.
Inputs may be any that keep to these rules, and one draw needn't show every extreme that they name: Each slab's live points are its first slab_counts slots; in every draw one slab is full with 1024. `grid_index`: every slot's point lies in the ball of radius 256 // 2 - 1 about the grid cell (128, 128, 128). `wavenumbers`: the columns are the 32 x 32 x 32 tensor grid of wavenumber triples, each exactly once, in some order.
All inputs are finite; a program needn't handle non-finite values.
Results may differ from the reference program's by a relative error of at most 0.002.
Values may be sent and summed in bfloat16 or wider, within the bound.
A program may use at most 192 MiB of HBM per device.

```python
import math
import jax
import jax.numpy as jnp
from jax import lax

KAXIS = 32
M = 32768
R = 256
G = 256
PERIOD = 512
CAP = 1024
P_SIZE = 8192
N_PT = 8


def draw_slab_counts(key, part):
    slab_index = jnp.arange(N_PT, dtype=jnp.int32)
    distance = jnp.abs(2 * slab_index + 1 - N_PT)
    nominal = CAP - distance * (3 * CAP // 4) // N_PT
    jitter = jax.random.randint(jax.random.fold_in(key, 1), (N_PT,), 0, CAP // 8 + 1)
    counts = jnp.maximum(nominal - jitter, CAP // 8)
    full_slab = jax.random.randint(jax.random.fold_in(key, 2), (), N_PT // 4, N_PT - N_PT // 4)
    return jnp.where(slab_index == full_slab, CAP, counts).astype(jnp.int32)


def draw_grid_index(key, part):
    middle = G // 2
    radius = G // 2 - 1
    candidates = jax.random.randint(jax.random.fold_in(key, 11), (8, 3, P_SIZE), 0, G).astype(jnp.int32)
    offsets = candidates - middle
    inside = (jnp.sum(offsets * offsets, axis=1) <= radius * radius).astype(jnp.int32)
    chosen = jnp.argmax(inside, axis=0).astype(jnp.int32)
    picked = jnp.take_along_axis(candidates, jnp.broadcast_to(chosen[None, None, :], (1, 3, P_SIZE)), axis=0)[0]
    fallback = candidates[0] // 2 + G // 4
    found = jnp.max(inside, axis=0) > 0
    return jnp.where(found[None, :], picked, fallback).astype(jnp.int32)


def draw_wavenumbers(key, part):
    order = jax.random.permutation(jax.random.fold_in(key, 21), M).astype(jnp.int32)
    rows = jnp.stack([order // (KAXIS * KAXIS), order // KAXIS % KAXIS, order % KAXIS], axis=0)
    return (rows - KAXIS // 2).astype(jnp.int32)


def with_ends(entries, own_key, low, high):
    longest = entries.shape.index(max(entries.shape))
    spots = []
    for shift in (0, 1):
        where = [jax.random.randint(jax.random.fold_in(own_key, axis), (), 0, length) for axis, length in enumerate(entries.shape)]
        where[longest] = (where[longest] + shift) % entries.shape[longest]
        spots.append(tuple(where))
    return entries.at[spots[0]].set(low).at[spots[1]].set(high)


def setup_inputs(seed: int = 0) -> dict:
    seeds = jax.random.split(jax.random.key(seed), 5)
    grid_index = draw_grid_index(jax.random.fold_in(seeds[4], 71), 0)
    wavenumbers = draw_wavenumbers(jax.random.fold_in(seeds[4], 71), 0)
    test_block = with_ends(jax.random.randint(seeds[2], (M, R), -64, 64), jax.random.fold_in(seeds[2], 1), -64, 63).astype(jnp.int32)
    slab_counts = draw_slab_counts(jax.random.fold_in(seeds[4], 71), 0)
    return {"grid_index": grid_index, "wavenumbers": wavenumbers, "test_block": test_block, "slab_counts": slab_counts}


def phase_pair(coords, wave_cols, in_use):
    turns = coords[0][:, None] * wave_cols[0][None, :] + coords[1][:, None] * wave_cols[1][None, :] + coords[2][:, None] * wave_cols[2][None, :]
    turns = jnp.mod(turns, PERIOD).astype(jnp.int32)
    angles = turns.astype(jnp.float32) * (2.0 * math.pi / PERIOD)
    tile_re = jnp.where(in_use[:, None], jnp.cos(angles), 0.0).astype(jnp.bfloat16)
    tile_im = jnp.where(in_use[:, None], jnp.sin(angles), 0.0).astype(jnp.bfloat16)
    return (tile_re, tile_im)

def reference(grid_index, wavenumbers, test_block, slab_counts):
    block = min(512, CAP)
    block_count = P_SIZE // block
    slots = jnp.arange(P_SIZE, dtype=jnp.int32)
    live_rows = slots % CAP < slab_counts[slots // CAP]
    test_float = test_block.astype(jnp.float32)
    hp = lax.Precision.HIGHEST
    y_scale = 1.0 / (32.0 * math.sqrt(M))
    w_scale = 1.0 / math.sqrt(P_SIZE)

    def tiles_of(step_index):
        first = (step_index * block).astype(jnp.int32)
        coords = lax.dynamic_slice(grid_index, (jnp.int32(0), first), (3, block))
        in_use = lax.dynamic_slice_in_dim(live_rows, first, block, 0)
        return phase_pair(coords, wavenumbers, in_use)

    def sketch_block(step_index):
        tile_re, tile_im = tiles_of(step_index)
        part_re = jnp.dot(tile_re.astype(jnp.float32), test_float, precision=hp)
        part_im = jnp.dot(tile_im.astype(jnp.float32), test_float, precision=hp)
        return (jnp.concatenate([part_re, part_im], axis=1) * y_scale).astype(jnp.bfloat16)
    sketch = lax.map(sketch_block, jnp.arange(block_count, dtype=jnp.int32)).reshape(P_SIZE, 2 * R)

    def adjoint_step(summed, step_index):
        tile_re, tile_im = tiles_of(step_index)
        rows = lax.dynamic_slice_in_dim(sketch, (step_index * block).astype(jnp.int32), block, 0).astype(jnp.float32)
        from_re = jnp.dot(tile_re.astype(jnp.float32).T, rows, precision=hp)
        from_im = jnp.dot(tile_im.astype(jnp.float32).T, rows, precision=hp)
        piece = jnp.concatenate([from_re[:, :R] + from_im[:, R:], from_re[:, R:] - from_im[:, :R]], axis=1)
        return (summed + piece, None)
    summed, unused = lax.scan(adjoint_step, jnp.zeros((M, 2 * R), jnp.float32), jnp.arange(block_count, dtype=jnp.int32))
    return summed * w_scale
```

```python
import functools
import math

import jax
import jax.numpy as jnp
from jax import lax
from jax.experimental import pallas as pl
from jax.experimental.pallas import tpu as pltpu
from jax.sharding import PartitionSpec as P

M = 32768
PERIOD = 512
DEPTH = 128
TILE = 256
STRIP = 32

S = (4.4428679, -7.3074434, 3.59478791, -0.78437358)
C = (1.41420408, -6.97764202, 5.71523797, -1.72834735)


def phases(whole_turns):
    r = whole_turns - jnp.round(whole_turns)
    z = r * r
    s = (((S[3] * z + S[2]) * z + S[1]) * z + S[0]) * r
    c = ((C[3] * z + C[2]) * z + C[1]) * z + C[0]
    return 1.0 - s * s, s * c


def sketch_kernel(count_ref, points_ref, waves_ref, test_ref, out_ref, turns_ref, lhs_ref):
    rows, width = out_ref.shape[0], test_ref.shape[1]

    @pl.when(pl.program_id(0) == 0)
    def _():
        out_ref[...] = jnp.zeros_like(out_ref)

    def block(index, carry):
        first = pl.multiple_of(index * TILE, TILE)
        total = None
        for k in range(test_ref.shape[0] // TILE):
            cols = pl.ds(k * TILE, TILE)
            turns_ref[k] = jnp.dot(
                points_ref[pl.ds(first, TILE), :], waves_ref[:, cols], preferred_element_type=jnp.float32
            )
            for j in range(TILE // STRIP):
                re, im = phases(turns_ref[k, pl.ds(j * STRIP, STRIP), :])
                lhs_ref[k, pl.ds(j * STRIP, STRIP), :] = re.astype(jnp.bfloat16)
                lhs_ref[k, pl.ds(TILE + j * STRIP, STRIP), :] = im.astype(jnp.bfloat16)
            test = test_ref[cols, :].astype(jnp.float32).astype(jnp.bfloat16)
            part = jnp.dot(lhs_ref[k], test, preferred_element_type=jnp.float32)
            total = part if total is None else total + part
        out_ref[pl.ds(first, TILE), pl.ds(0, width)] += total[:TILE]
        out_ref[pl.ds(first, TILE), pl.ds(width, width)] += total[TILE:]
        return carry

    lax.fori_loop(0, (count_ref[0] + TILE - 1) // TILE, block, 0)


def adjoint_kernel(scale, counts_ref, waves_ref, points_ref, sketch_ref, out_ref, turns_ref, lhs_ref, rhs_ref):
    modes, width = out_ref.shape[0], sketch_ref.shape[1] // 2
    slab = pl.program_id(0)

    @pl.when(slab == 0)
    def _():
        out_ref[...] = jnp.zeros_like(out_ref)

    def block(index, carry):
        first = pl.multiple_of(index * TILE, TILE)
        rhs_ref[pl.ds(0, TILE), :] = sketch_ref[pl.ds(first, TILE), :]
        rhs_ref[pl.ds(TILE, TILE), pl.ds(0, width)] = sketch_ref[pl.ds(first, TILE), pl.ds(width, width)]
        rhs_ref[pl.ds(TILE, TILE), pl.ds(width, width)] = -sketch_ref[pl.ds(first, TILE), pl.ds(0, width)]
        for k in range(modes // TILE):
            rows = pl.ds(k * TILE, TILE)
            turns_ref[k] = jnp.dot(
                waves_ref[rows, :], points_ref[:, pl.ds(first, TILE)], preferred_element_type=jnp.float32
            )
            for j in range(TILE // STRIP):
                re, im = phases(turns_ref[k, pl.ds(j * STRIP, STRIP), :])
                lhs_ref[k, pl.ds(j * STRIP, STRIP), pl.ds(0, TILE)] = re.astype(jnp.bfloat16)
                lhs_ref[k, pl.ds(j * STRIP, STRIP), pl.ds(TILE, TILE)] = im.astype(jnp.bfloat16)
            out_ref[rows, :] += jnp.dot(lhs_ref[k], rhs_ref[...], preferred_element_type=jnp.float32)
        return carry

    lax.fori_loop(0, (counts_ref[slab] + TILE - 1) // TILE, block, 0)

    @pl.when(slab == pl.num_programs(0) - 1)
    def _():
        out_ref[...] = out_ref[...] * scale


def padded(rows, factor):
    rows = rows.astype(jnp.float32) * factor
    return jnp.pad(rows, ((0, DEPTH - rows.shape[0]), (0, 0))).astype(jnp.bfloat16)


def sketch_part(count, points, waves, test_block):
    rows, modes, width = points.shape[0], waves.shape[1], test_block.shape[1]
    step = 1024
    return pl.pallas_call(
        sketch_kernel,
        out_shape=jax.ShapeDtypeStruct((rows, 2 * width), jnp.float32),
        grid=(modes // step,),
        in_specs=[
            pl.BlockSpec(memory_space=pltpu.SMEM),
            pl.BlockSpec((rows, DEPTH), lambda m: (0, 0)),
            pl.BlockSpec((DEPTH, step), lambda m: (0, m)),
            pl.BlockSpec((step, width), lambda m: (m, 0)),
        ],
        out_specs=pl.BlockSpec((rows, 2 * width), lambda m: (0, 0)),
        scratch_shapes=[
            pltpu.VMEM((step // TILE, TILE, TILE), jnp.float32),
            pltpu.VMEM((step // TILE, 2 * TILE, TILE), jnp.bfloat16),
        ],
        compiler_params=pltpu.CompilerParams(vmem_limit_bytes=40 * 2**20),
        cost_estimate=pl.CostEstimate(
            flops=4 * rows * modes * width, bytes_accessed=4 * modes * width, transcendentals=0
        ),
    )(count, points, waves, test_block)


def adjoint_part(scale, counts, waves, points, sketch, capacity):
    modes, slots, width = waves.shape[0], points.shape[1], sketch.shape[1]
    return pl.pallas_call(
        functools.partial(adjoint_kernel, scale),
        out_shape=jax.ShapeDtypeStruct((modes, width), jnp.float32),
        grid=(slots // capacity,),
        in_specs=[
            pl.BlockSpec(memory_space=pltpu.SMEM),
            pl.BlockSpec((modes, DEPTH), lambda p: (0, 0)),
            pl.BlockSpec((DEPTH, capacity), lambda p: (0, p)),
            pl.BlockSpec((capacity, width), lambda p: (p, 0)),
        ],
        out_specs=pl.BlockSpec((modes, width), lambda p: (0, 0)),
        scratch_shapes=[
            pltpu.VMEM((modes // TILE, TILE, TILE), jnp.float32),
            pltpu.VMEM((modes // TILE, TILE, 2 * TILE), jnp.bfloat16),
            pltpu.VMEM((2 * TILE, width), jnp.bfloat16),
        ],
        compiler_params=pltpu.CompilerParams(vmem_limit_bytes=40 * 2**20),
        cost_estimate=pl.CostEstimate(
            flops=4 * modes * slots * width, bytes_accessed=2 * slots * width, transcendentals=0
        ),
    )(counts, waves, points, sketch)


def per_device(grid_index, wavenumbers, test_block, slab_counts):
    capacity = grid_index.shape[1]
    n_pt = lax.axis_size("pt")
    y_scale = 1.0 / (32.0 * math.sqrt(M))
    w_scale = 1.0 / math.sqrt(capacity * n_pt)
    counts = lax.all_gather(slab_counts, "pt", tiled=True)
    all_points = lax.all_gather(grid_index, "pt", axis=1, tiled=True)
    points = padded(grid_index, 1.0)
    waves = padded(wavenumbers, 1.0 / PERIOD)
    partial_value = sketch_part(slab_counts, points.T, waves, test_block)
    quarter = lax.psum_scatter(partial_value, "md", scatter_dimension=0, tiled=True)
    rows = quarter.shape[0]
    slot = lax.axis_index("md") * rows + jnp.arange(rows, dtype=jnp.int32)
    quarter = jnp.where((slot < slab_counts[0])[:, None], quarter * y_scale, 0.0).astype(jnp.bfloat16)
    sketch = lax.all_gather(quarter, ("pt", "md"), tiled=True)
    own = wavenumbers.shape[1] // n_pt
    mine = lax.dynamic_slice_in_dim(waves, lax.axis_index("pt") * own, own, 1)
    return adjoint_part(w_scale, counts, mine.T, padded(all_points, 1.0), sketch, capacity)


def solution(mesh):
    placed = (P(None, "pt"), P(None, "md"), P("md", None), P("pt"))
    return jax.shard_map(
        per_device, mesh=mesh, in_specs=placed, out_specs=P(("md", "pt"), None), check_vma=False
    )
```

```python
import functools
import math

import jax
import jax.numpy as jnp
from jax import lax
from jax.experimental import pallas as pl
from jax.experimental.pallas import tpu as pltpu
from jax.sharding import PartitionSpec as P

M = 32768
PERIOD = 512
DEPTH = 128
TILE = 256
STRIP = 32

S = (4.4428679, -7.3074434, 3.59478791, -0.78437358)
C = (1.41420408, -6.97764202, 5.71523797, -1.72834735)


def phases(whole_turns):
    r = whole_turns - jnp.round(whole_turns)
    z = r * r
    s = (((S[3] * z + S[2]) * z + S[1]) * z + S[0]) * r
    c = ((C[3] * z + C[2]) * z + C[1]) * z + C[0]
    return 1.0 - s * s, s * c


def sketch_kernel(dtype, count_ref, points_ref, waves_ref, test_ref, result_ref, turns_ref, lhs_ref, out_ref):
    rows, width = out_ref.shape[0], test_ref.shape[1]

    @pl.when(pl.program_id(0) == 0)
    def _():
        out_ref[...] = jnp.zeros_like(out_ref)

    def block(index, carry):
        first = pl.multiple_of(index * TILE, TILE)
        total = None
        for k in range(test_ref.shape[0] // TILE):
            cols = pl.ds(k * TILE, TILE)
            turns_ref[k] = jnp.dot(
                points_ref[pl.ds(first, TILE), :], waves_ref[:, cols], preferred_element_type=jnp.float32
            )
            for j in range(TILE // STRIP):
                re, im = phases(turns_ref[k, pl.ds(j * STRIP, STRIP), :])
                lhs_ref[k, pl.ds(j * STRIP, STRIP), :] = re.astype(jnp.bfloat16)
                lhs_ref[k, pl.ds(TILE + j * STRIP, STRIP), :] = im.astype(jnp.bfloat16)
            test = test_ref[cols, :].astype(jnp.float32).astype(jnp.bfloat16)
            part = jnp.dot(lhs_ref[k], test, preferred_element_type=jnp.float32)
            total = part if total is None else total + part
        out_ref[pl.ds(first, TILE), pl.ds(0, width)] += total[:TILE]
        out_ref[pl.ds(first, TILE), pl.ds(width, width)] += total[TILE:]
        return carry

    lax.fori_loop(0, (count_ref[0] + TILE - 1) // TILE, block, 0)

    @pl.when(pl.program_id(0) == pl.num_programs(0) - 1)
    def _():
        slot = lax.broadcasted_iota(jnp.int32, out_ref.shape, 0)
        result_ref[...] = jnp.where(slot < count_ref[0], out_ref[...], 0.0).astype(dtype)


def adjoint_kernel(scale, counts_ref, waves_ref, points_ref, sketch_ref, out_ref, turns_ref, lhs_ref, rhs_ref):
    modes, width = out_ref.shape[0], sketch_ref.shape[1] // 2
    slab = pl.program_id(0)

    @pl.when(slab == 0)
    def _():
        out_ref[...] = jnp.zeros_like(out_ref)

    def block(index, carry):
        first = pl.multiple_of(index * TILE, TILE)
        rhs_ref[pl.ds(0, TILE), :] = sketch_ref[pl.ds(first, TILE), :]
        rhs_ref[pl.ds(TILE, TILE), pl.ds(0, width)] = sketch_ref[pl.ds(first, TILE), pl.ds(width, width)]
        rhs_ref[pl.ds(TILE, TILE), pl.ds(width, width)] = -sketch_ref[pl.ds(first, TILE), pl.ds(0, width)]
        for k in range(modes // TILE):
            rows = pl.ds(k * TILE, TILE)
            turns_ref[k] = jnp.dot(
                waves_ref[rows, :], points_ref[:, pl.ds(first, TILE)], preferred_element_type=jnp.float32
            )
            for j in range(TILE // STRIP):
                re, im = phases(turns_ref[k, pl.ds(j * STRIP, STRIP), :])
                lhs_ref[k, pl.ds(j * STRIP, STRIP), pl.ds(0, TILE)] = re.astype(jnp.bfloat16)
                lhs_ref[k, pl.ds(j * STRIP, STRIP), pl.ds(TILE, TILE)] = im.astype(jnp.bfloat16)
            out_ref[rows, :] += jnp.dot(lhs_ref[k], rhs_ref[...], preferred_element_type=jnp.float32)
        return carry

    lax.fori_loop(0, (counts_ref[slab] + TILE - 1) // TILE, block, 0)

    @pl.when(slab == pl.num_programs(0) - 1)
    def _():
        out_ref[...] = out_ref[...] * scale


def padded(rows, factor):
    rows = rows.astype(jnp.float32) * factor
    return jnp.pad(rows, ((0, DEPTH - rows.shape[0]), (0, 0))).astype(jnp.bfloat16)


def sketch_part(count, points, waves, test_block, dtype):
    rows, modes, width = points.shape[0], waves.shape[1], test_block.shape[1]
    step = 1024
    return pl.pallas_call(
        functools.partial(sketch_kernel, dtype),
        out_shape=jax.ShapeDtypeStruct((rows, 2 * width), dtype),
        grid=(modes // step,),
        in_specs=[
            pl.BlockSpec(memory_space=pltpu.SMEM),
            pl.BlockSpec((rows, DEPTH), lambda m: (0, 0)),
            pl.BlockSpec((DEPTH, step), lambda m: (0, m)),
            pl.BlockSpec((step, width), lambda m: (m, 0)),
        ],
        out_specs=pl.BlockSpec((rows, 2 * width), lambda m: (0, 0)),
        scratch_shapes=[
            pltpu.VMEM((step // TILE, TILE, TILE), jnp.float32),
            pltpu.VMEM((step // TILE, 2 * TILE, TILE), jnp.bfloat16),
            pltpu.VMEM((rows, 2 * width), jnp.float32),
        ],
        compiler_params=pltpu.CompilerParams(vmem_limit_bytes=40 * 2**20),
        cost_estimate=pl.CostEstimate(
            flops=4 * rows * modes * width, bytes_accessed=4 * modes * width, transcendentals=0
        ),
    )(count, points, waves, test_block)


def adjoint_part(scale, counts, waves, points, sketch, capacity):
    modes, slots, width = waves.shape[0], points.shape[1], sketch.shape[1]
    return pl.pallas_call(
        functools.partial(adjoint_kernel, scale),
        out_shape=jax.ShapeDtypeStruct((modes, width), jnp.float32),
        grid=(slots // capacity,),
        in_specs=[
            pl.BlockSpec(memory_space=pltpu.SMEM),
            pl.BlockSpec((modes, DEPTH), lambda p: (0, 0)),
            pl.BlockSpec((DEPTH, capacity), lambda p: (0, p)),
            pl.BlockSpec((capacity, width), lambda p: (p, 0)),
        ],
        out_specs=pl.BlockSpec((modes, width), lambda p: (0, 0)),
        scratch_shapes=[
            pltpu.VMEM((modes // TILE, TILE, TILE), jnp.float32),
            pltpu.VMEM((modes // TILE, TILE, 2 * TILE), jnp.bfloat16),
            pltpu.VMEM((2 * TILE, width), jnp.bfloat16),
        ],
        compiler_params=pltpu.CompilerParams(vmem_limit_bytes=40 * 2**20),
        cost_estimate=pl.CostEstimate(
            flops=4 * modes * slots * width, bytes_accessed=2 * slots * width, transcendentals=0
        ),
    )(counts, waves, points, sketch)


def exchange_kernel(
    scale, part_ref, info_ref, out_ref, all_ref, landed_ref,
    sum_out, sum_in, z_out, z_in, x_out, x_in, y_out, y_in, core_out, core_in, info_out, info_in,
):
    pt, md = lax.axis_index("pt"), lax.axis_index("md")
    rows = part_ref.shape[0]
    quarter = rows // 4
    core, x, y = pt % 2, (pt // 2) % 2, pt // 4
    core_pt, x_pt, y_pt = pt + 1 - 2 * core, pt + 2 - 4 * x, pt + 4 - 8 * y
    xy_pt = x_pt + 4 - 8 * y

    def send(source, target, out_sem, in_sem, to_pt, to_md):
        copy = pltpu.make_async_remote_copy(
            src_ref=source, dst_ref=target, send_sem=out_sem, recv_sem=in_sem,
            device_id=(to_pt, to_md), device_id_type=pl.DeviceIdType.MESH,
        )
        copy.start()
        return copy

    def place(slab, part):
        return out_ref.at[pl.ds(pl.multiple_of(slab * rows + part * quarter, quarter), quarter), :]

    barrier = pltpu.get_barrier_semaphore()
    for d in range(1, 4):
        pl.semaphore_signal(
            barrier, inc=1, device_id=(pt, (md + d) % 4), device_id_type=pl.DeviceIdType.MESH
        )
    for d in range(1, 8):
        pl.semaphore_signal(
            barrier, inc=1, device_id=((pt + d) % 8, md), device_id_type=pl.DeviceIdType.MESH
        )
    pl.semaphore_wait(barrier, 10)

    sums = []
    for d in (2, 1, 3):
        to = (md + d) % 4
        source = part_ref.at[pl.ds(pl.multiple_of(to * quarter, quarter), quarter), :]
        sums.append(send(source, landed_ref.at[d - 1], sum_out.at[d - 1], sum_in.at[d - 1], pt, to))
    others = [
        send(info_ref, all_ref.at[pt], info_out.at[d - 1], info_in.at[d - 1], (pt + d) % 8, md)
        for d in range(1, 8)
    ]
    all_ref[pt] = info_ref[...]
    for copy in sums:
        copy.wait_recv()
    total = part_ref[pl.ds(pl.multiple_of(md * quarter, quarter), quarter), :].astype(jnp.float32)
    for d in range(3):
        total = total + landed_ref[d].astype(jnp.float32)
    place(pt, md)[...] = (total * scale).astype(jnp.bfloat16)

    own = place(pt, md)
    ups = [send(own, own, z_out.at[d - 1], z_in.at[d - 1], pt, (md + d) % 4) for d in (1, 2, 3)]
    pieces = [md, (md + 3) % 4, (md + 2) % 4, (md + 1) % 4]
    over_x, over_y, over_core = [], [], []
    for d in range(4):
        if d:
            ups[d - 1].wait_recv()
        here = place(pt, pieces[d])
        over_x.append(send(here, here, x_out.at[d], x_in.at[d], x_pt, md))
        over_y.append(send(here, here, y_out.at[d], y_in.at[d], y_pt, md))
        over_core.append(send(here, here, core_out.at[d], core_in.at[d], core_pt, md))
    forward_x, forward_y = [], []
    for d in range(4):
        over_x[d].wait_recv()
        here = place(x_pt, pieces[d])
        if d < 2:
            forward_y.append(send(here, here, y_out.at[4 + d], y_in.at[4 + d], y_pt, md))
        over_core.append(send(here, here, core_out.at[4 + d], core_in.at[4 + d], core_pt, md))
        over_y[d].wait_recv()
        here = place(y_pt, pieces[d])
        if d >= 2:
            forward_x.append(send(here, here, x_out.at[2 + d], x_in.at[2 + d], x_pt, md))
        over_core.append(send(here, here, core_out.at[8 + d], core_in.at[8 + d], core_pt, md))
    for d in range(4):
        (forward_y[d] if d < 2 else forward_x[d - 2]).wait_recv()
        here = place(xy_pt, pieces[d])
        over_core.append(send(here, here, core_out.at[12 + d], core_in.at[12 + d], core_pt, md))
    for copy in over_core + others:
        copy.wait_recv()
    for copy in sums + others + ups + over_x + over_y + over_core + forward_x + forward_y:
        copy.wait_send()


def exchange(scale, part, info):
    rows, width = part.shape
    sems = [n for n in (3, 3, 6, 6, 16, 7) for _ in range(2)]
    return pl.pallas_call(
        functools.partial(exchange_kernel, scale),
        out_shape=(
            jax.ShapeDtypeStruct((8 * rows, width), jnp.bfloat16),
            jax.ShapeDtypeStruct((8,) + info.shape, info.dtype),
        ),
        in_specs=[pl.BlockSpec(memory_space=pltpu.VMEM)] * 2,
        out_specs=(pl.BlockSpec(memory_space=pltpu.VMEM),) * 2,
        scratch_shapes=[pltpu.VMEM((3, rows // 4, width), jnp.bfloat16)]
        + [pltpu.SemaphoreType.DMA((n,)) for n in sems],
        compiler_params=pltpu.CompilerParams(
            collective_id=0, has_side_effects=True, vmem_limit_bytes=24 * 2**20
        ),
    )(part, info)


def per_device(grid_index, wavenumbers, test_block, slab_counts):
    capacity = grid_index.shape[1]
    n_pt, n_md = lax.axis_size("pt"), lax.axis_size("md")
    y_scale = 1.0 / (32.0 * math.sqrt(M))
    w_scale = 1.0 / math.sqrt(capacity * n_pt)
    points = padded(grid_index, 1.0)
    waves = padded(wavenumbers, 1.0 / PERIOD)
    if (n_pt, n_md) == (8, 4):
        part = sketch_part(slab_counts, points.T, waves, test_block, jnp.bfloat16)
        info = jnp.concatenate(
            [grid_index, jnp.broadcast_to(slab_counts[:, None], (5, capacity))], axis=0
        )
        sketch, gathered = exchange(y_scale, part, info)
        counts = gathered[:, 3, 0]
        all_points = gathered[:, :3, :].transpose(1, 0, 2).reshape(3, n_pt * capacity)
    else:
        counts = lax.all_gather(slab_counts, "pt", tiled=True)
        all_points = lax.all_gather(grid_index, "pt", axis=1, tiled=True)
        part = sketch_part(slab_counts, points.T, waves, test_block, jnp.float32)
        share = lax.psum_scatter(part, "md", scatter_dimension=0, tiled=True)
        share = (share * y_scale).astype(jnp.bfloat16)
        sketch = lax.all_gather(share, ("pt", "md"), tiled=True)
    own = wavenumbers.shape[1] // n_pt
    mine = lax.dynamic_slice_in_dim(waves, lax.axis_index("pt") * own, own, 1)
    return adjoint_part(w_scale, counts, mine.T, padded(all_points, 1.0), sketch, capacity)


def solution(mesh):
    placed = (P(None, "pt"), P(None, "md"), P("md", None), P("pt"))
    return jax.shard_map(
        per_device, mesh=mesh, in_specs=placed, out_specs=P(("md", "pt"), None), check_vma=False
    )
```

```python
import functools
import math

import jax
import jax.numpy as jnp
from jax import lax
from jax.experimental import pallas as pl
from jax.experimental.pallas import tpu as pltpu
from jax.sharding import PartitionSpec as P

M = 32768
PERIOD = 512
DEPTH = 128
TILE = 256
STRIP = 32
MARKS = (10, 11, 13, 15, 17, 20, 23, 26, 29)

S = (4.4428679, -7.3074434, 3.59478791, -0.78437358)
C = (1.41420408, -6.97764202, 5.71523797, -1.72834735)


def phases(whole_turns):
    r = whole_turns - jnp.round(whole_turns)
    z = r * r
    s = (((S[3] * z + S[2]) * z + S[1]) * z + S[0]) * r
    c = ((C[3] * z + C[2]) * z + C[1]) * z + C[0]
    return 1.0 - s * s, s * c


def sketch_kernel(dtype, count_ref, points_ref, waves_ref, test_ref, result_ref, turns_ref, lhs_ref, out_ref):
    rows, width = out_ref.shape[0], test_ref.shape[1]

    @pl.when(pl.program_id(0) == 0)
    def _():
        out_ref[...] = jnp.zeros_like(out_ref)

    def block(index, carry):
        first = pl.multiple_of(index * TILE, TILE)
        total = None
        for k in range(test_ref.shape[0] // TILE):
            cols = pl.ds(k * TILE, TILE)
            turns_ref[k] = jnp.dot(
                points_ref[pl.ds(first, TILE), :], waves_ref[:, cols], preferred_element_type=jnp.float32
            )
            for j in range(TILE // STRIP):
                re, im = phases(turns_ref[k, pl.ds(j * STRIP, STRIP), :])
                lhs_ref[k, pl.ds(j * STRIP, STRIP), :] = re.astype(jnp.bfloat16)
                lhs_ref[k, pl.ds(TILE + j * STRIP, STRIP), :] = im.astype(jnp.bfloat16)
            test = test_ref[cols, :].astype(jnp.float32).astype(jnp.bfloat16)
            part = jnp.dot(lhs_ref[k], test, preferred_element_type=jnp.float32)
            total = part if total is None else total + part
        out_ref[pl.ds(first, TILE), pl.ds(0, width)] += total[:TILE]
        out_ref[pl.ds(first, TILE), pl.ds(width, width)] += total[TILE:]
        return carry

    lax.fori_loop(0, (count_ref[0] + TILE - 1) // TILE, block, 0)

    @pl.when(pl.program_id(0) == pl.num_programs(0) - 1)
    def _():
        slot = lax.broadcasted_iota(jnp.int32, out_ref.shape, 0)
        result_ref[...] = jnp.where(slot < count_ref[0], out_ref[...], 0.0).astype(dtype)


def adjoint_kernel(scale, counts_ref, waves_ref, points_ref, sketch_ref, out_ref, turns_ref, lhs_ref, rhs_ref):
    modes, width = out_ref.shape[0], sketch_ref.shape[1] // 2
    slab = pl.program_id(0)

    @pl.when(slab == 0)
    def _():
        out_ref[...] = jnp.zeros_like(out_ref)

    def block(index, carry):
        first = pl.multiple_of(index * TILE, TILE)
        rhs_ref[pl.ds(0, TILE), :] = sketch_ref[pl.ds(first, TILE), :]
        rhs_ref[pl.ds(TILE, TILE), pl.ds(0, width)] = sketch_ref[pl.ds(first, TILE), pl.ds(width, width)]
        rhs_ref[pl.ds(TILE, TILE), pl.ds(width, width)] = -sketch_ref[pl.ds(first, TILE), pl.ds(0, width)]
        for k in range(modes // TILE):
            rows = pl.ds(k * TILE, TILE)
            turns_ref[k] = jnp.dot(
                waves_ref[rows, :], points_ref[:, pl.ds(first, TILE)], preferred_element_type=jnp.float32
            )
            for j in range(TILE // STRIP):
                re, im = phases(turns_ref[k, pl.ds(j * STRIP, STRIP), :])
                lhs_ref[k, pl.ds(j * STRIP, STRIP), pl.ds(0, TILE)] = re.astype(jnp.bfloat16)
                lhs_ref[k, pl.ds(j * STRIP, STRIP), pl.ds(TILE, TILE)] = im.astype(jnp.bfloat16)
            out_ref[rows, :] += jnp.dot(lhs_ref[k], rhs_ref[...], preferred_element_type=jnp.float32)
        return carry

    lax.fori_loop(0, (counts_ref[slab] + TILE - 1) // TILE, block, 0)

    @pl.when(slab == pl.num_programs(0) - 1)
    def _():
        out_ref[...] = out_ref[...] * scale


def product_kernel(scale, live_ref, phase_ref, sketch_ref, out_ref, rhs_ref):
    width = sketch_ref.shape[1] // 2
    step = pl.program_id(0)

    @pl.when(step == 0)
    def _():
        out_ref[...] = jnp.zeros_like(out_ref)

    @pl.when(step < live_ref[0])
    def _():
        rhs_ref[pl.ds(0, TILE), :] = sketch_ref[...]
        rhs_ref[pl.ds(TILE, TILE), pl.ds(0, width)] = sketch_ref[:, pl.ds(width, width)]
        rhs_ref[pl.ds(TILE, TILE), pl.ds(width, width)] = -sketch_ref[:, pl.ds(0, width)]
        out_ref[...] += jnp.dot(phase_ref[0], rhs_ref[...], preferred_element_type=jnp.float32)

    @pl.when(step == pl.num_programs(0) - 1)
    def _():
        out_ref[...] = out_ref[...] * scale


def product(scale, live, order, phase, sketch):
    blocks, modes, _ = phase.shape
    width = sketch.shape[1]
    return pl.pallas_call(
        lambda live_ref, order_ref, *refs: product_kernel(scale, live_ref, *refs),
        out_shape=jax.ShapeDtypeStruct((modes, width), jnp.float32),
        grid_spec=pltpu.PrefetchScalarGridSpec(
            num_scalar_prefetch=2,
            grid=(blocks,),
            in_specs=[
                pl.BlockSpec((1, modes, 2 * TILE), lambda b, live, order: (order[b], 0, 0)),
                pl.BlockSpec((TILE, width), lambda b, live, order: (order[b], 0)),
            ],
            out_specs=pl.BlockSpec((modes, width), lambda b, live, order: (0, 0)),
            scratch_shapes=[pltpu.VMEM((2 * TILE, width), jnp.bfloat16)],
        ),
        compiler_params=pltpu.CompilerParams(vmem_limit_bytes=24 * 2**20),
    )(live, order, phase, sketch)


def padded(rows, factor):
    rows = rows.astype(jnp.float32) * factor
    return jnp.pad(rows, ((0, DEPTH - rows.shape[0]), (0, 0))).astype(jnp.bfloat16)


def sketch_part(count, points, waves, test_block, dtype):
    rows, modes, width = points.shape[0], waves.shape[1], test_block.shape[1]
    step = 1024
    return pl.pallas_call(
        functools.partial(sketch_kernel, dtype),
        out_shape=jax.ShapeDtypeStruct((rows, 2 * width), dtype),
        grid=(modes // step,),
        in_specs=[
            pl.BlockSpec(memory_space=pltpu.SMEM),
            pl.BlockSpec((rows, DEPTH), lambda m: (0, 0)),
            pl.BlockSpec((DEPTH, step), lambda m: (0, m)),
            pl.BlockSpec((step, width), lambda m: (m, 0)),
        ],
        out_specs=pl.BlockSpec((rows, 2 * width), lambda m: (0, 0)),
        scratch_shapes=[
            pltpu.VMEM((step // TILE, TILE, TILE), jnp.float32),
            pltpu.VMEM((step // TILE, 2 * TILE, TILE), jnp.bfloat16),
            pltpu.VMEM((rows, 2 * width), jnp.float32),
        ],
        compiler_params=pltpu.CompilerParams(vmem_limit_bytes=40 * 2**20),
        cost_estimate=pl.CostEstimate(
            flops=4 * rows * modes * width, bytes_accessed=4 * modes * width, transcendentals=0
        ),
    )(count, points, waves, test_block)


def adjoint_part(scale, counts, waves, points, sketch, capacity):
    modes, slots, width = waves.shape[0], points.shape[1], sketch.shape[1]
    return pl.pallas_call(
        functools.partial(adjoint_kernel, scale),
        out_shape=jax.ShapeDtypeStruct((modes, width), jnp.float32),
        grid=(slots // capacity,),
        in_specs=[
            pl.BlockSpec(memory_space=pltpu.SMEM),
            pl.BlockSpec((modes, DEPTH), lambda p: (0, 0)),
            pl.BlockSpec((DEPTH, capacity), lambda p: (0, p)),
            pl.BlockSpec((capacity, width), lambda p: (p, 0)),
        ],
        out_specs=pl.BlockSpec((modes, width), lambda p: (0, 0)),
        scratch_shapes=[
            pltpu.VMEM((modes // TILE, TILE, TILE), jnp.float32),
            pltpu.VMEM((modes // TILE, TILE, 2 * TILE), jnp.bfloat16),
            pltpu.VMEM((2 * TILE, width), jnp.bfloat16),
        ],
        compiler_params=pltpu.CompilerParams(vmem_limit_bytes=40 * 2**20),
        cost_estimate=pl.CostEstimate(
            flops=4 * modes * slots * width, bytes_accessed=2 * slots * width, transcendentals=0
        ),
    )(counts, waves, points, sketch)


def exchange_kernel(
    scale, part_ref, info_ref, waves_ref, out_ref, all_ref, phase_ref, landed_ref, points_ref, turns_ref, made_ref, made_sem,
    sum_out, sum_in, z_out, z_in, x_out, x_in, y_out, y_in, core_out, core_in, info_out, info_in,
):
    pt, md = lax.axis_index("pt"), lax.axis_index("md")
    rows = part_ref.shape[0]
    quarter = rows // 4
    core, x, y = pt % 2, (pt // 2) % 2, pt // 4
    core_pt, x_pt, y_pt = pt + 1 - 2 * core, pt + 2 - 4 * x, pt + 4 - 8 * y
    xy_pt = x_pt + 4 - 8 * y

    def send(source, target, out_sem, in_sem, to_pt, to_md):
        copy = pltpu.make_async_remote_copy(
            src_ref=source, dst_ref=target, send_sem=out_sem, recv_sem=in_sem,
            device_id=(to_pt, to_md), device_id_type=pl.DeviceIdType.MESH,
        )
        copy.start()
        return copy

    def place(slab, part):
        return out_ref.at[pl.ds(pl.multiple_of(slab * rows + part * quarter, quarter), quarter), :]

    barrier = pltpu.get_barrier_semaphore()
    for d in range(1, 4):
        pl.semaphore_signal(
            barrier, inc=1, device_id=(pt, (md + d) % 4), device_id_type=pl.DeviceIdType.MESH
        )
    for d in range(1, 8):
        pl.semaphore_signal(
            barrier, inc=1, device_id=((pt + d) % 8, md), device_id_type=pl.DeviceIdType.MESH
        )
    pl.semaphore_wait(barrier, 10)

    sums = []
    for d in (2, 1, 3):
        to = (md + d) % 4
        source = part_ref.at[pl.ds(pl.multiple_of(to * quarter, quarter), quarter), :]
        sums.append(send(source, landed_ref.at[d - 1], sum_out.at[d - 1], sum_in.at[d - 1], pt, to))
    others = [
        send(info_ref, all_ref.at[pt], info_out.at[d - 1], info_in.at[d - 1], (pt + d) % 8, md)
        for d in range(1, 8)
    ]
    all_ref[pt] = info_ref[...]
    for copy in others:
        copy.wait_recv()
    points_ref[...] = jnp.zeros_like(points_ref)
    for slab in range(8):
        points_ref[pl.ds(0, 8), pl.ds(slab * rows, rows)] = all_ref[slab].astype(jnp.float32)

    def keep(index):
        slot = index % 2
        return pltpu.make_async_copy(made_ref.at[slot], phase_ref.at[index], made_sem.at[slot])

    def make(first, last):
        def body(index, carry):
            slot = index % 2
            start = pl.multiple_of(index * TILE, TILE)
            coords = points_ref[:, pl.ds(start, TILE)].astype(jnp.bfloat16)

            if first >= 2:
                keep(index - 2).wait()
            for k in range(waves_ref.shape[0] // TILE):
                turns_ref[k] = jnp.dot(
                    waves_ref[pl.ds(k * TILE, TILE), :], coords, preferred_element_type=jnp.float32
                )
                for j in range(TILE // STRIP):
                    re, im = phases(turns_ref[k, pl.ds(j * STRIP, STRIP), :])
                    at = pl.ds(k * TILE + j * STRIP, STRIP)
                    made_ref[slot, at, pl.ds(0, TILE)] = re.astype(jnp.bfloat16)
                    made_ref[slot, at, pl.ds(TILE, TILE)] = im.astype(jnp.bfloat16)
            keep(index).start()
            return carry

        lax.fori_loop(first, last, body, 0)

    make(0, 2)
    make(2, MARKS[0])
    for copy in sums:
        copy.wait_recv()
    total = part_ref[pl.ds(pl.multiple_of(md * quarter, quarter), quarter), :].astype(jnp.float32)
    for d in range(3):
        total = total + landed_ref[d].astype(jnp.float32)
    place(pt, md)[...] = (total * scale).astype(jnp.bfloat16)

    own = place(pt, md)
    ups = [send(own, own, z_out.at[d - 1], z_in.at[d - 1], pt, (md + d) % 4) for d in (1, 2, 3)]
    pieces = [md, (md + 3) % 4, (md + 2) % 4, (md + 1) % 4]
    over_x, over_y, over_core = [], [], []
    for d in range(4):
        if d:
            ups[d - 1].wait_recv()
        here = place(pt, pieces[d])
        over_x.append(send(here, here, x_out.at[d], x_in.at[d], x_pt, md))
        over_y.append(send(here, here, y_out.at[d], y_in.at[d], y_pt, md))
        over_core.append(send(here, here, core_out.at[d], core_in.at[d], core_pt, md))
        make(MARKS[d], MARKS[d + 1])
    forward_x, forward_y = [], []
    for d in range(4):
        over_x[d].wait_recv()
        here = place(x_pt, pieces[d])
        if d < 2:
            forward_y.append(send(here, here, y_out.at[4 + d], y_in.at[4 + d], y_pt, md))
        over_core.append(send(here, here, core_out.at[4 + d], core_in.at[4 + d], core_pt, md))
        over_y[d].wait_recv()
        here = place(y_pt, pieces[d])
        if d >= 2:
            forward_x.append(send(here, here, x_out.at[2 + d], x_in.at[2 + d], x_pt, md))
        over_core.append(send(here, here, core_out.at[8 + d], core_in.at[8 + d], core_pt, md))
        make(MARKS[4 + d], MARKS[5 + d])
    for d in range(4):
        (forward_y[d] if d < 2 else forward_x[d - 2]).wait_recv()
        here = place(xy_pt, pieces[d])
        over_core.append(send(here, here, core_out.at[12 + d], core_in.at[12 + d], core_pt, md))
    make(MARKS[8], phase_ref.shape[0])
    keep(phase_ref.shape[0] - 2).wait()
    keep(phase_ref.shape[0] - 1).wait()
    for copy in over_core:
        copy.wait_recv()
    for copy in sums + others + ups + over_x + over_y + over_core + forward_x + forward_y:
        copy.wait_send()


def exchange(scale, part, info, waves):
    rows, width = part.shape
    modes = waves.shape[0]
    sems = [n for n in (3, 3, 6, 6, 16, 7) for _ in range(2)]
    return pl.pallas_call(
        functools.partial(exchange_kernel, scale),
        out_shape=(
            jax.ShapeDtypeStruct((8 * rows, width), jnp.bfloat16),
            jax.ShapeDtypeStruct((8,) + info.shape, info.dtype),
            jax.ShapeDtypeStruct((8 * rows // TILE, modes, 2 * TILE), jnp.bfloat16),
        ),
        in_specs=[pl.BlockSpec(memory_space=pltpu.VMEM)] * 3,
        out_specs=(pl.BlockSpec(memory_space=pltpu.VMEM),) * 2 + (pl.BlockSpec(memory_space=pl.ANY),),
        scratch_shapes=[
            pltpu.VMEM((3, rows // 4, width), jnp.bfloat16),
            pltpu.VMEM((DEPTH, 8 * rows), jnp.float32),
            pltpu.VMEM((modes // TILE, TILE, TILE), jnp.float32),
            pltpu.VMEM((2, modes, 2 * TILE), jnp.bfloat16),
            pltpu.SemaphoreType.DMA((2,)),
        ]
        + [pltpu.SemaphoreType.DMA((n,)) for n in sems],
        compiler_params=pltpu.CompilerParams(
            collective_id=0, has_side_effects=True, vmem_limit_bytes=32 * 2**20
        ),
    )(part, info, waves)


def per_device(grid_index, wavenumbers, test_block, slab_counts):
    capacity = grid_index.shape[1]
    n_pt, n_md = lax.axis_size("pt"), lax.axis_size("md")
    y_scale = 1.0 / (32.0 * math.sqrt(M))
    w_scale = 1.0 / math.sqrt(capacity * n_pt)
    points = padded(grid_index, 1.0)
    waves = padded(wavenumbers, 1.0 / PERIOD)
    own = wavenumbers.shape[1] // n_pt
    mine = lax.dynamic_slice_in_dim(waves, lax.axis_index("pt") * own, own, 1)
    if (n_pt, n_md) == (8, 4):
        part = sketch_part(slab_counts, points.T, waves, test_block, jnp.bfloat16)
        info = jnp.concatenate(
            [grid_index, jnp.broadcast_to(slab_counts[:, None], (5, capacity))], axis=0
        )
        sketch, gathered, phase = exchange(y_scale, part, info, mine.T)
        per_slab = (gathered[:, 3, 0] + TILE - 1) // TILE
        ends = jnp.sum(jnp.where(jnp.arange(8)[:, None] <= jnp.arange(8)[None, :], per_slab[:, None], 0), axis=0)
        nth = jnp.minimum(jnp.arange(phase.shape[0], dtype=jnp.int32), ends[7] - 1)
        past = (ends[None, :] <= nth[:, None]).astype(jnp.int32)
        slab = jnp.sum(past, axis=1)
        order = slab * (capacity // TILE) + nth - jnp.sum(past * per_slab[None, :], axis=1)
        return product(w_scale, ends[7:], order.astype(jnp.int32), phase, sketch)
    else:
        counts = lax.all_gather(slab_counts, "pt", tiled=True)
        all_points = lax.all_gather(grid_index, "pt", axis=1, tiled=True)
        part = sketch_part(slab_counts, points.T, waves, test_block, jnp.float32)
        share = lax.psum_scatter(part, "md", scatter_dimension=0, tiled=True)
        share = (share * y_scale).astype(jnp.bfloat16)
        sketch = lax.all_gather(share, ("pt", "md"), tiled=True)
    return adjoint_part(w_scale, counts, mine.T, padded(all_points, 1.0), sketch, capacity)


def solution(mesh):
    placed = (P(None, "pt"), P(None, "md"), P("md", None), P("pt"))
    return jax.shard_map(
        per_device, mesh=mesh, in_specs=placed, out_specs=P(("md", "pt"), None), check_vma=False
    )
```

```python
import functools
import math

import jax
import jax.numpy as jnp
from jax import lax
from jax.experimental import pallas as pl
from jax.experimental.pallas import tpu as pltpu
from jax.sharding import PartitionSpec as P

M = 32768
PERIOD = 512
DEPTH = 128
TILE = 256
STRIP = 32
SKETCH = (2048, 512, 512)
MARKS = (10, 11, 13, 15, 17, 20, 23, 26, 29)

S = (4.4428679, -7.3074434, 3.59478791, -0.78437358)
C = (1.41420408, -6.97764202, 5.71523797, -1.72834735)


def phases(whole_turns):
    r = whole_turns - jnp.round(whole_turns)
    z = r * r
    s = (((S[3] * z + S[2]) * z + S[1]) * z + S[0]) * r
    c = ((C[3] * z + C[2]) * z + C[1]) * z + C[0]
    return 1.0 - s * s, s * c


def sketch_kernel(
    dtype, count_ref, points_ref, waves_ref, test_ref, result_ref, turns_ref, lhs_ref, out_ref, cast_ref
):
    width, tile, step = test_ref.shape[1], turns_ref.shape[1], test_ref.shape[0]
    chunk = turns_ref.shape[2]

    @pl.when(pl.program_id(0) == 0)
    def _():
        out_ref[...] = jnp.zeros_like(out_ref)

    cast_ref[...] = test_ref[...].astype(jnp.float32).astype(jnp.bfloat16)

    def block(index, carry):
        first = pl.multiple_of(index * tile, tile)
        for k in range(step // chunk):
            cols = pl.ds(k * chunk, chunk)
            turns_ref[k] = jnp.dot(
                points_ref[pl.ds(first, tile), :], waves_ref[:, cols], preferred_element_type=jnp.float32
            )
            for j in range(tile // STRIP):
                re, im = phases(turns_ref[k, pl.ds(j * STRIP, STRIP), :])
                lhs_ref[pl.ds(j * STRIP, STRIP), cols] = re.astype(jnp.bfloat16)
                lhs_ref[pl.ds(tile + j * STRIP, STRIP), cols] = im.astype(jnp.bfloat16)
        total = jnp.dot(lhs_ref[...], cast_ref[...], preferred_element_type=jnp.float32)
        out_ref[pl.ds(first, tile), pl.ds(0, width)] += total[:tile]
        out_ref[pl.ds(first, tile), pl.ds(width, width)] += total[tile:]
        return carry

    lax.fori_loop(0, (count_ref[0] + tile - 1) // tile, block, 0)

    @pl.when(pl.program_id(0) == pl.num_programs(0) - 1)
    def _():
        slot = lax.broadcasted_iota(jnp.int32, out_ref.shape, 0)
        result_ref[...] = jnp.where(slot < count_ref[0], out_ref[...], 0.0).astype(dtype)


def adjoint_kernel(scale, counts_ref, waves_ref, points_ref, sketch_ref, out_ref, turns_ref, lhs_ref, rhs_ref):
    modes, width = out_ref.shape[0], sketch_ref.shape[1] // 2
    slab = pl.program_id(0)

    @pl.when(slab == 0)
    def _():
        out_ref[...] = jnp.zeros_like(out_ref)

    def block(index, carry):
        first = pl.multiple_of(index * TILE, TILE)
        rhs_ref[pl.ds(0, TILE), :] = sketch_ref[pl.ds(first, TILE), :]
        rhs_ref[pl.ds(TILE, TILE), pl.ds(0, width)] = sketch_ref[pl.ds(first, TILE), pl.ds(width, width)]
        rhs_ref[pl.ds(TILE, TILE), pl.ds(width, width)] = -sketch_ref[pl.ds(first, TILE), pl.ds(0, width)]
        for k in range(modes // TILE):
            rows = pl.ds(k * TILE, TILE)
            turns_ref[k] = jnp.dot(
                waves_ref[rows, :], points_ref[:, pl.ds(first, TILE)], preferred_element_type=jnp.float32
            )
            for j in range(TILE // STRIP):
                re, im = phases(turns_ref[k, pl.ds(j * STRIP, STRIP), :])
                lhs_ref[k, pl.ds(j * STRIP, STRIP), pl.ds(0, TILE)] = re.astype(jnp.bfloat16)
                lhs_ref[k, pl.ds(j * STRIP, STRIP), pl.ds(TILE, TILE)] = im.astype(jnp.bfloat16)
            out_ref[rows, :] += jnp.dot(lhs_ref[k], rhs_ref[...], preferred_element_type=jnp.float32)
        return carry

    lax.fori_loop(0, (counts_ref[slab] + TILE - 1) // TILE, block, 0)

    @pl.when(slab == pl.num_programs(0) - 1)
    def _():
        out_ref[...] = out_ref[...] * scale


def product_kernel(scale, live_ref, first_ref, second_ref, upper_ref, lower_ref, out_ref, rhs_ref):
    width = upper_ref.shape[1] // 2
    step = pl.program_id(0)

    @pl.when(step == 0)
    def _():
        out_ref[...] = jnp.zeros_like(out_ref)

    @pl.when(2 * step < live_ref[0])
    def _():
        upper, lower = upper_ref[...], lower_ref[...]
        lower = jnp.where(2 * step + 1 < live_ref[0], lower, jnp.zeros_like(lower))
        for g, rows in enumerate((upper, lower)):
            rhs_ref[pl.ds(2 * g * TILE, TILE), :] = rows
            rhs_ref[pl.ds((2 * g + 1) * TILE, TILE), pl.ds(0, width)] = rows[:, width:]
            rhs_ref[pl.ds((2 * g + 1) * TILE, TILE), pl.ds(width, width)] = -rows[:, :width]
        lhs = jnp.concatenate([first_ref[0], second_ref[0]], axis=1)
        out_ref[...] += jnp.dot(lhs, rhs_ref[...], preferred_element_type=jnp.float32)

    @pl.when(step == pl.num_programs(0) - 1)
    def _():
        out_ref[...] = out_ref[...] * scale


def product(scale, live, order, phase, sketch):
    blocks, modes, _ = phase.shape
    width = sketch.shape[1]
    return pl.pallas_call(
        lambda live_ref, order_ref, *refs: product_kernel(scale, live_ref, *refs),
        out_shape=jax.ShapeDtypeStruct((modes, width), jnp.float32),
        grid_spec=pltpu.PrefetchScalarGridSpec(
            num_scalar_prefetch=2,
            grid=(blocks // 2,),
            in_specs=[
                pl.BlockSpec((1, modes, 2 * TILE), lambda b, live, order: (order[2 * b], 0, 0)),
                pl.BlockSpec((1, modes, 2 * TILE), lambda b, live, order: (order[2 * b + 1], 0, 0)),
                pl.BlockSpec((TILE, width), lambda b, live, order: (order[2 * b], 0)),
                pl.BlockSpec((TILE, width), lambda b, live, order: (order[2 * b + 1], 0)),
            ],
            out_specs=pl.BlockSpec((modes, width), lambda b, live, order: (0, 0)),
            scratch_shapes=[pltpu.VMEM((4 * TILE, width), jnp.bfloat16)],
        ),
        compiler_params=pltpu.CompilerParams(vmem_limit_bytes=30 * 2**20),
    )(live, order, phase, phase, sketch, sketch)


def padded(rows, factor):
    rows = rows.astype(jnp.float32) * factor
    return jnp.pad(rows, ((0, DEPTH - rows.shape[0]), (0, 0))).astype(jnp.bfloat16)


def sketch_part(count, points, waves, test_block, dtype):
    rows, modes, width = points.shape[0], waves.shape[1], test_block.shape[1]
    step, tile, chunk = SKETCH
    return pl.pallas_call(
        functools.partial(sketch_kernel, dtype),
        out_shape=jax.ShapeDtypeStruct((rows, 2 * width), dtype),
        grid=(modes // step,),
        in_specs=[
            pl.BlockSpec(memory_space=pltpu.SMEM),
            pl.BlockSpec((rows, DEPTH), lambda m: (0, 0)),
            pl.BlockSpec((DEPTH, step), lambda m: (0, m)),
            pl.BlockSpec((step, width), lambda m: (m, 0)),
        ],
        out_specs=pl.BlockSpec((rows, 2 * width), lambda m: (0, 0)),
        scratch_shapes=[
            pltpu.VMEM((step // chunk, tile, chunk), jnp.float32),
            pltpu.VMEM((2 * tile, step), jnp.bfloat16),
            pltpu.VMEM((rows, 2 * width), jnp.float32),
            pltpu.VMEM((step, width), jnp.bfloat16),
        ],
        compiler_params=pltpu.CompilerParams(vmem_limit_bytes=40 * 2**20),
        cost_estimate=pl.CostEstimate(
            flops=4 * rows * modes * width, bytes_accessed=4 * modes * width, transcendentals=0
        ),
    )(count, points, waves, test_block)


def adjoint_part(scale, counts, waves, points, sketch, capacity):
    modes, slots, width = waves.shape[0], points.shape[1], sketch.shape[1]
    return pl.pallas_call(
        functools.partial(adjoint_kernel, scale),
        out_shape=jax.ShapeDtypeStruct((modes, width), jnp.float32),
        grid=(slots // capacity,),
        in_specs=[
            pl.BlockSpec(memory_space=pltpu.SMEM),
            pl.BlockSpec((modes, DEPTH), lambda p: (0, 0)),
            pl.BlockSpec((DEPTH, capacity), lambda p: (0, p)),
            pl.BlockSpec((capacity, width), lambda p: (p, 0)),
        ],
        out_specs=pl.BlockSpec((modes, width), lambda p: (0, 0)),
        scratch_shapes=[
            pltpu.VMEM((modes // TILE, TILE, TILE), jnp.float32),
            pltpu.VMEM((modes // TILE, TILE, 2 * TILE), jnp.bfloat16),
            pltpu.VMEM((2 * TILE, width), jnp.bfloat16),
        ],
        compiler_params=pltpu.CompilerParams(vmem_limit_bytes=40 * 2**20),
        cost_estimate=pl.CostEstimate(
            flops=4 * modes * slots * width, bytes_accessed=2 * slots * width, transcendentals=0
        ),
    )(counts, waves, points, sketch)


def exchange_kernel(
    scale, part_ref, info_ref, waves_ref, out_ref, all_ref, phase_ref, landed_ref, points_ref, turns_ref, made_ref, made_sem,
    sum_out, sum_in, z_out, z_in, x_out, x_in, y_out, y_in, core_out, core_in, info_out, info_in,
):
    pt, md = lax.axis_index("pt"), lax.axis_index("md")
    rows = part_ref.shape[0]
    quarter = rows // 4
    core, x, y = pt % 2, (pt // 2) % 2, pt // 4
    core_pt, x_pt, y_pt = pt + 1 - 2 * core, pt + 2 - 4 * x, pt + 4 - 8 * y
    xy_pt = x_pt + 4 - 8 * y

    def send(source, target, out_sem, in_sem, to_pt, to_md):
        copy = pltpu.make_async_remote_copy(
            src_ref=source, dst_ref=target, send_sem=out_sem, recv_sem=in_sem,
            device_id=(to_pt, to_md), device_id_type=pl.DeviceIdType.MESH,
        )
        copy.start()
        return copy

    def place(slab, part):
        return out_ref.at[pl.ds(pl.multiple_of(slab * rows + part * quarter, quarter), quarter), :]

    barrier = pltpu.get_barrier_semaphore()
    for d in range(1, 4):
        pl.semaphore_signal(
            barrier, inc=1, device_id=(pt, (md + d) % 4), device_id_type=pl.DeviceIdType.MESH
        )
    for d in range(1, 8):
        pl.semaphore_signal(
            barrier, inc=1, device_id=((pt + d) % 8, md), device_id_type=pl.DeviceIdType.MESH
        )
    pl.semaphore_wait(barrier, 10)

    sums = []
    for d in (2, 1, 3):
        to = (md + d) % 4
        source = part_ref.at[pl.ds(pl.multiple_of(to * quarter, quarter), quarter), :]
        sums.append(send(source, landed_ref.at[d - 1], sum_out.at[d - 1], sum_in.at[d - 1], pt, to))
    others = [
        send(info_ref, all_ref.at[pt], info_out.at[d - 1], info_in.at[d - 1], (pt + d) % 8, md)
        for d in range(1, 8)
    ]
    all_ref[pt] = info_ref[...]
    for copy in others:
        copy.wait_recv()
    points_ref[...] = jnp.zeros_like(points_ref)
    for slab in range(8):
        points_ref[pl.ds(0, 8), pl.ds(slab * rows, rows)] = all_ref[slab].astype(jnp.float32)

    def keep(index):
        slot = index % 2
        return pltpu.make_async_copy(made_ref.at[slot], phase_ref.at[index], made_sem.at[slot])

    def make(first, last):
        def body(index, carry):
            slot = index % 2
            start = pl.multiple_of(index * TILE, TILE)
            coords = points_ref[:, pl.ds(start, TILE)].astype(jnp.bfloat16)

            if first >= 2:
                keep(index - 2).wait()
            for k in range(waves_ref.shape[0] // TILE):
                turns_ref[k] = jnp.dot(
                    waves_ref[pl.ds(k * TILE, TILE), :], coords, preferred_element_type=jnp.float32
                )
                for j in range(TILE // STRIP):
                    re, im = phases(turns_ref[k, pl.ds(j * STRIP, STRIP), :])
                    at = pl.ds(k * TILE + j * STRIP, STRIP)
                    made_ref[slot, at, pl.ds(0, TILE)] = re.astype(jnp.bfloat16)
                    made_ref[slot, at, pl.ds(TILE, TILE)] = im.astype(jnp.bfloat16)
            keep(index).start()
            return carry

        lax.fori_loop(first, last, body, 0)

    make(0, 2)
    make(2, MARKS[0])
    for copy in sums:
        copy.wait_recv()
    total = part_ref[pl.ds(pl.multiple_of(md * quarter, quarter), quarter), :].astype(jnp.float32)
    for d in range(3):
        total = total + landed_ref[d].astype(jnp.float32)
    place(pt, md)[...] = (total * scale).astype(jnp.bfloat16)

    own = place(pt, md)
    ups = [send(own, own, z_out.at[d - 1], z_in.at[d - 1], pt, (md + d) % 4) for d in (1, 2, 3)]
    pieces = [md, (md + 3) % 4, (md + 2) % 4, (md + 1) % 4]
    over_x, over_y, over_core = [], [], []
    for d in range(4):
        if d:
            ups[d - 1].wait_recv()
        here = place(pt, pieces[d])
        over_x.append(send(here, here, x_out.at[d], x_in.at[d], x_pt, md))
        over_y.append(send(here, here, y_out.at[d], y_in.at[d], y_pt, md))
        over_core.append(send(here, here, core_out.at[d], core_in.at[d], core_pt, md))
        make(MARKS[d], MARKS[d + 1])
    forward_x, forward_y = [], []
    for d in range(4):
        over_x[d].wait_recv()
        here = place(x_pt, pieces[d])
        if d < 2:
            forward_y.append(send(here, here, y_out.at[4 + d], y_in.at[4 + d], y_pt, md))
        over_core.append(send(here, here, core_out.at[4 + d], core_in.at[4 + d], core_pt, md))
        over_y[d].wait_recv()
        here = place(y_pt, pieces[d])
        if d >= 2:
            forward_x.append(send(here, here, x_out.at[2 + d], x_in.at[2 + d], x_pt, md))
        over_core.append(send(here, here, core_out.at[8 + d], core_in.at[8 + d], core_pt, md))
        make(MARKS[4 + d], MARKS[5 + d])
    for d in range(4):
        (forward_y[d] if d < 2 else forward_x[d - 2]).wait_recv()
        here = place(xy_pt, pieces[d])
        over_core.append(send(here, here, core_out.at[12 + d], core_in.at[12 + d], core_pt, md))
    make(MARKS[8], phase_ref.shape[0])
    keep(phase_ref.shape[0] - 2).wait()
    keep(phase_ref.shape[0] - 1).wait()
    for copy in over_core:
        copy.wait_recv()
    for copy in sums + others + ups + over_x + over_y + over_core + forward_x + forward_y:
        copy.wait_send()


def exchange(scale, part, info, waves):
    rows, width = part.shape
    modes = waves.shape[0]
    sems = [n for n in (3, 3, 6, 6, 16, 7) for _ in range(2)]
    return pl.pallas_call(
        functools.partial(exchange_kernel, scale),
        out_shape=(
            jax.ShapeDtypeStruct((8 * rows, width), jnp.bfloat16),
            jax.ShapeDtypeStruct((8,) + info.shape, info.dtype),
            jax.ShapeDtypeStruct((8 * rows // TILE, modes, 2 * TILE), jnp.bfloat16),
        ),
        in_specs=[pl.BlockSpec(memory_space=pltpu.VMEM)] * 3,
        out_specs=(pl.BlockSpec(memory_space=pltpu.VMEM),) * 2 + (pl.BlockSpec(memory_space=pl.ANY),),
        scratch_shapes=[
            pltpu.VMEM((3, rows // 4, width), jnp.bfloat16),
            pltpu.VMEM((DEPTH, 8 * rows), jnp.float32),
            pltpu.VMEM((modes // TILE, TILE, TILE), jnp.float32),
            pltpu.VMEM((2, modes, 2 * TILE), jnp.bfloat16),
            pltpu.SemaphoreType.DMA((2,)),
        ]
        + [pltpu.SemaphoreType.DMA((n,)) for n in sems],
        compiler_params=pltpu.CompilerParams(
            collective_id=0, has_side_effects=True, vmem_limit_bytes=32 * 2**20
        ),
    )(part, info, waves)


def per_device(grid_index, wavenumbers, test_block, slab_counts):
    capacity = grid_index.shape[1]
    n_pt, n_md = lax.axis_size("pt"), lax.axis_size("md")
    y_scale = 1.0 / (32.0 * math.sqrt(M))
    w_scale = 1.0 / math.sqrt(capacity * n_pt)
    points = padded(grid_index, 1.0)
    waves = padded(wavenumbers, 1.0 / PERIOD)
    own = wavenumbers.shape[1] // n_pt
    mine = lax.dynamic_slice_in_dim(waves, lax.axis_index("pt") * own, own, 1)
    if (n_pt, n_md) == (8, 4):
        part = sketch_part(slab_counts, points.T, waves, test_block, jnp.bfloat16)
        info = jnp.concatenate(
            [grid_index, jnp.broadcast_to(slab_counts[:, None], (5, capacity))], axis=0
        )
        sketch, gathered, phase = exchange(y_scale, part, info, mine.T)
        per_slab = (gathered[:, 3, 0] + TILE - 1) // TILE
        ends = jnp.sum(jnp.where(jnp.arange(8)[:, None] <= jnp.arange(8)[None, :], per_slab[:, None], 0), axis=0)
        nth = jnp.minimum(jnp.arange(phase.shape[0], dtype=jnp.int32), ends[7] - 1)
        past = (ends[None, :] <= nth[:, None]).astype(jnp.int32)
        slab = jnp.sum(past, axis=1)
        order = slab * (capacity // TILE) + nth - jnp.sum(past * per_slab[None, :], axis=1)
        return product(w_scale, ends[7:], order.astype(jnp.int32), phase, sketch)
    else:
        counts = lax.all_gather(slab_counts, "pt", tiled=True)
        all_points = lax.all_gather(grid_index, "pt", axis=1, tiled=True)
        part = sketch_part(slab_counts, points.T, waves, test_block, jnp.float32)
        share = lax.psum_scatter(part, "md", scatter_dimension=0, tiled=True)
        share = (share * y_scale).astype(jnp.bfloat16)
        sketch = lax.all_gather(share, ("pt", "md"), tiled=True)
    return adjoint_part(w_scale, counts, mine.T, padded(all_points, 1.0), sketch, capacity)


def solution(mesh):
    placed = (P(None, "pt"), P(None, "md"), P("md", None), P("pt"))
    return jax.shard_map(
        per_device, mesh=mesh, in_specs=placed, out_specs=P(("md", "pt"), None), check_vma=False
    )
```

```python
import functools
import math

import jax
import jax.numpy as jnp
from jax import lax
from jax.experimental import pallas as pl
from jax.experimental.pallas import tpu as pltpu
from jax.sharding import PartitionSpec as P

M = 32768
PERIOD = 512
DEPTH = 128
TILE = 256
STRIP = 32
SKETCH = (2048, 512, 512)
MARKS = (10, 11, 13, 15, 17, 20, 23, 26, 29)

S = (4.4428679, -7.3074434, 3.59478791, -0.78437358)
C = (1.41420408, -6.97764202, 5.71523797, -1.72834735)


def phases(whole_turns):
    r = whole_turns - jnp.round(whole_turns)
    z = r * r
    s = (((S[3] * z + S[2]) * z + S[1]) * z + S[0]) * r
    c = ((C[3] * z + C[2]) * z + C[1]) * z + C[0]
    return 1.0 - s * s, s * c


def sketch_kernel(
    dtype, count_ref, points_ref, waves_ref, test_ref, result_ref, turns_ref, lhs_ref, out_ref, cast_ref
):
    width, tile, step = test_ref.shape[1], turns_ref.shape[1], test_ref.shape[0]
    chunk = turns_ref.shape[2]

    @pl.when(pl.program_id(0) == 0)
    def _():
        out_ref[...] = jnp.zeros_like(out_ref)

    cast_ref[...] = test_ref[...].astype(jnp.float32).astype(jnp.bfloat16)

    def block(index, carry):
        first = pl.multiple_of(index * tile, tile)
        for k in range(step // chunk):
            cols = pl.ds(k * chunk, chunk)
            turns_ref[k] = jnp.dot(
                points_ref[pl.ds(first, tile), :], waves_ref[:, cols], preferred_element_type=jnp.float32
            )
            for j in range(tile // STRIP):
                re, im = phases(turns_ref[k, pl.ds(j * STRIP, STRIP), :])
                lhs_ref[pl.ds(j * STRIP, STRIP), cols] = re.astype(jnp.bfloat16)
                lhs_ref[pl.ds(tile + j * STRIP, STRIP), cols] = im.astype(jnp.bfloat16)
        total = jnp.dot(lhs_ref[...], cast_ref[...], preferred_element_type=jnp.float32)
        out_ref[pl.ds(first, tile), pl.ds(0, width)] += total[:tile]
        out_ref[pl.ds(first, tile), pl.ds(width, width)] += total[tile:]
        return carry

    lax.fori_loop(0, (count_ref[0] + tile - 1) // tile, block, 0)

    @pl.when(pl.program_id(0) == pl.num_programs(0) - 1)
    def _():
        slot = lax.broadcasted_iota(jnp.int32, out_ref.shape, 0)
        result_ref[...] = jnp.where(slot < count_ref[0], out_ref[...], 0.0).astype(dtype)


def adjoint_kernel(scale, counts_ref, waves_ref, points_ref, sketch_ref, out_ref, turns_ref, lhs_ref, rhs_ref):
    modes, width = out_ref.shape[0], sketch_ref.shape[1] // 2
    slab = pl.program_id(0)

    @pl.when(slab == 0)
    def _():
        out_ref[...] = jnp.zeros_like(out_ref)

    def block(index, carry):
        first = pl.multiple_of(index * TILE, TILE)
        rhs_ref[pl.ds(0, TILE), :] = sketch_ref[pl.ds(first, TILE), :]
        rhs_ref[pl.ds(TILE, TILE), pl.ds(0, width)] = sketch_ref[pl.ds(first, TILE), pl.ds(width, width)]
        rhs_ref[pl.ds(TILE, TILE), pl.ds(width, width)] = -sketch_ref[pl.ds(first, TILE), pl.ds(0, width)]
        for k in range(modes // TILE):
            rows = pl.ds(k * TILE, TILE)
            turns_ref[k] = jnp.dot(
                waves_ref[rows, :], points_ref[:, pl.ds(first, TILE)], preferred_element_type=jnp.float32
            )
            for j in range(TILE // STRIP):
                re, im = phases(turns_ref[k, pl.ds(j * STRIP, STRIP), :])
                lhs_ref[k, pl.ds(j * STRIP, STRIP), pl.ds(0, TILE)] = re.astype(jnp.bfloat16)
                lhs_ref[k, pl.ds(j * STRIP, STRIP), pl.ds(TILE, TILE)] = im.astype(jnp.bfloat16)
            out_ref[rows, :] += jnp.dot(lhs_ref[k], rhs_ref[...], preferred_element_type=jnp.float32)
        return carry

    lax.fori_loop(0, (counts_ref[slab] + TILE - 1) // TILE, block, 0)

    @pl.when(slab == pl.num_programs(0) - 1)
    def _():
        out_ref[...] = out_ref[...] * scale


def product_kernel(scale, live_ref, first_ref, second_ref, upper_ref, lower_ref, out_ref, rhs_ref):
    width = upper_ref.shape[1] // 2
    step = pl.program_id(0)

    @pl.when(step == 0)
    def _():
        out_ref[...] = jnp.zeros_like(out_ref)

    @pl.when(2 * step < live_ref[0])
    def _():
        upper, lower = upper_ref[...], lower_ref[...]
        lower = jnp.where(2 * step + 1 < live_ref[0], lower, jnp.zeros_like(lower))
        for g, rows in enumerate((upper, lower)):
            rhs_ref[pl.ds(2 * g * TILE, TILE), :] = rows
            rhs_ref[pl.ds((2 * g + 1) * TILE, TILE), pl.ds(0, width)] = rows[:, width:]
            rhs_ref[pl.ds((2 * g + 1) * TILE, TILE), pl.ds(width, width)] = -rows[:, :width]
        lhs = jnp.concatenate([first_ref[0], second_ref[0]], axis=1)
        out_ref[...] += jnp.dot(lhs, rhs_ref[...], preferred_element_type=jnp.float32)

    @pl.when(step == pl.num_programs(0) - 1)
    def _():
        out_ref[...] = out_ref[...] * scale


def product(scale, live, order, phase, sketch):
    blocks, modes, _ = phase.shape
    width = sketch.shape[1]
    return pl.pallas_call(
        lambda live_ref, order_ref, *refs: product_kernel(scale, live_ref, *refs),
        out_shape=jax.ShapeDtypeStruct((modes, width), jnp.float32),
        grid_spec=pltpu.PrefetchScalarGridSpec(
            num_scalar_prefetch=2,
            grid=(blocks // 2,),
            in_specs=[
                pl.BlockSpec((1, modes, 2 * TILE), lambda b, live, order: (order[2 * b], 0, 0)),
                pl.BlockSpec((1, modes, 2 * TILE), lambda b, live, order: (order[2 * b + 1], 0, 0)),
                pl.BlockSpec((TILE, width), lambda b, live, order: (order[2 * b], 0)),
                pl.BlockSpec((TILE, width), lambda b, live, order: (order[2 * b + 1], 0)),
            ],
            out_specs=pl.BlockSpec((modes, width), lambda b, live, order: (0, 0)),
            scratch_shapes=[pltpu.VMEM((4 * TILE, width), jnp.bfloat16)],
        ),
        compiler_params=pltpu.CompilerParams(vmem_limit_bytes=30 * 2**20),
    )(live, order, phase, phase, sketch, sketch)


def padded(rows, factor):
    rows = rows.astype(jnp.float32) * factor
    return jnp.pad(rows, ((0, DEPTH - rows.shape[0]), (0, 0))).astype(jnp.bfloat16)


def sketch_part(count, points, waves, test_block, dtype):
    rows, modes, width = points.shape[0], waves.shape[1], test_block.shape[1]
    step, tile, chunk = SKETCH
    return pl.pallas_call(
        functools.partial(sketch_kernel, dtype),
        out_shape=jax.ShapeDtypeStruct((rows, 2 * width), dtype),
        grid=(modes // step,),
        in_specs=[
            pl.BlockSpec(memory_space=pltpu.SMEM),
            pl.BlockSpec((rows, DEPTH), lambda m: (0, 0)),
            pl.BlockSpec((DEPTH, step), lambda m: (0, m)),
            pl.BlockSpec((step, width), lambda m: (m, 0)),
        ],
        out_specs=pl.BlockSpec((rows, 2 * width), lambda m: (0, 0)),
        scratch_shapes=[
            pltpu.VMEM((step // chunk, tile, chunk), jnp.float32),
            pltpu.VMEM((2 * tile, step), jnp.bfloat16),
            pltpu.VMEM((rows, 2 * width), jnp.float32),
            pltpu.VMEM((step, width), jnp.bfloat16),
        ],
        compiler_params=pltpu.CompilerParams(vmem_limit_bytes=58 * 2**20),
        cost_estimate=pl.CostEstimate(
            flops=4 * rows * modes * width, bytes_accessed=4 * modes * width, transcendentals=0
        ),
    )(count, points, waves, test_block)


def adjoint_part(scale, counts, waves, points, sketch, capacity):
    modes, slots, width = waves.shape[0], points.shape[1], sketch.shape[1]
    return pl.pallas_call(
        functools.partial(adjoint_kernel, scale),
        out_shape=jax.ShapeDtypeStruct((modes, width), jnp.float32),
        grid=(slots // capacity,),
        in_specs=[
            pl.BlockSpec(memory_space=pltpu.SMEM),
            pl.BlockSpec((modes, DEPTH), lambda p: (0, 0)),
            pl.BlockSpec((DEPTH, capacity), lambda p: (0, p)),
            pl.BlockSpec((capacity, width), lambda p: (p, 0)),
        ],
        out_specs=pl.BlockSpec((modes, width), lambda p: (0, 0)),
        scratch_shapes=[
            pltpu.VMEM((modes // TILE, TILE, TILE), jnp.float32),
            pltpu.VMEM((modes // TILE, TILE, 2 * TILE), jnp.bfloat16),
            pltpu.VMEM((2 * TILE, width), jnp.bfloat16),
        ],
        compiler_params=pltpu.CompilerParams(vmem_limit_bytes=40 * 2**20),
        cost_estimate=pl.CostEstimate(
            flops=4 * modes * slots * width, bytes_accessed=2 * slots * width, transcendentals=0
        ),
    )(counts, waves, points, sketch)


def exchange_kernel(
    scale, part_ref, info_ref, waves_ref, out_ref, all_ref, phase_ref, landed_ref, points_ref, turns_ref, made_ref, made_sem,
    sum_out, sum_in, z_out, z_in, x_out, x_in, y_out, y_in, core_out, core_in, info_out, info_in,
):
    pt, md = lax.axis_index("pt"), lax.axis_index("md")
    rows = part_ref.shape[0]
    quarter = rows // 4
    core, x, y = pt % 2, (pt // 2) % 2, pt // 4
    core_pt, x_pt, y_pt = pt + 1 - 2 * core, pt + 2 - 4 * x, pt + 4 - 8 * y
    xy_pt = x_pt + 4 - 8 * y

    def send(source, target, out_sem, in_sem, to_pt, to_md):
        copy = pltpu.make_async_remote_copy(
            src_ref=source, dst_ref=target, send_sem=out_sem, recv_sem=in_sem,
            device_id=(to_pt, to_md), device_id_type=pl.DeviceIdType.MESH,
        )
        copy.start()
        return copy

    def place(slab, part):
        return out_ref.at[pl.ds(pl.multiple_of(slab * rows + part * quarter, quarter), quarter), :]

    barrier = pltpu.get_barrier_semaphore()
    for d in range(1, 4):
        pl.semaphore_signal(
            barrier, inc=1, device_id=(pt, (md + d) % 4), device_id_type=pl.DeviceIdType.MESH
        )
    for d in range(1, 8):
        pl.semaphore_signal(
            barrier, inc=1, device_id=((pt + d) % 8, md), device_id_type=pl.DeviceIdType.MESH
        )
    pl.semaphore_wait(barrier, 10)

    sums = []
    for d in (2, 1, 3):
        to = (md + d) % 4
        source = part_ref.at[pl.ds(pl.multiple_of(to * quarter, quarter), quarter), :]
        sums.append(send(source, landed_ref.at[d - 1], sum_out.at[d - 1], sum_in.at[d - 1], pt, to))
    others = [
        send(info_ref, all_ref.at[pt], info_out.at[d - 1], info_in.at[d - 1], (pt + d) % 8, md)
        for d in range(1, 8)
    ]
    all_ref[pt] = info_ref[...]
    for copy in others:
        copy.wait_recv()
    points_ref[...] = jnp.zeros_like(points_ref)
    for slab in range(8):
        points_ref[pl.ds(0, 8), pl.ds(slab * rows, rows)] = all_ref[slab].astype(jnp.float32)

    def keep(index):
        slot = index % 2
        return pltpu.make_async_copy(made_ref.at[slot], phase_ref.at[index], made_sem.at[slot])

    def make(first, last):
        def body(index, carry):
            slot = index % 2
            start = pl.multiple_of(index * TILE, TILE)
            coords = points_ref[:, pl.ds(start, TILE)].astype(jnp.bfloat16)

            if first >= 2:
                keep(index - 2).wait()
            for k in range(waves_ref.shape[0] // TILE):
                turns_ref[k] = jnp.dot(
                    waves_ref[pl.ds(k * TILE, TILE), :], coords, preferred_element_type=jnp.float32
                )
                for j in range(TILE // STRIP):
                    re, im = phases(turns_ref[k, pl.ds(j * STRIP, STRIP), :])
                    at = pl.ds(k * TILE + j * STRIP, STRIP)
                    made_ref[slot, at, pl.ds(0, TILE)] = re.astype(jnp.bfloat16)
                    made_ref[slot, at, pl.ds(TILE, TILE)] = im.astype(jnp.bfloat16)
            keep(index).start()
            return carry

        lax.fori_loop(first, last, body, 0)

    make(0, 2)
    make(2, MARKS[0])
    for copy in sums:
        copy.wait_recv()
    total = part_ref[pl.ds(pl.multiple_of(md * quarter, quarter), quarter), :].astype(jnp.float32)
    for d in range(3):
        total = total + landed_ref[d].astype(jnp.float32)
    place(pt, md)[...] = (total * scale).astype(jnp.bfloat16)

    own = place(pt, md)
    ups = [send(own, own, z_out.at[d - 1], z_in.at[d - 1], pt, (md + d) % 4) for d in (1, 2, 3)]
    pieces = [md, (md + 3) % 4, (md + 2) % 4, (md + 1) % 4]
    over_x, over_y, over_core = [], [], []
    for d in range(4):
        if d:
            ups[d - 1].wait_recv()
        here = place(pt, pieces[d])
        over_x.append(send(here, here, x_out.at[d], x_in.at[d], x_pt, md))
        over_y.append(send(here, here, y_out.at[d], y_in.at[d], y_pt, md))
        over_core.append(send(here, here, core_out.at[d], core_in.at[d], core_pt, md))
        make(MARKS[d], MARKS[d + 1])
    forward_x, forward_y = [], []
    for d in range(4):
        over_x[d].wait_recv()
        here = place(x_pt, pieces[d])
        if d < 2:
            forward_y.append(send(here, here, y_out.at[4 + d], y_in.at[4 + d], y_pt, md))
        over_core.append(send(here, here, core_out.at[4 + d], core_in.at[4 + d], core_pt, md))
        over_y[d].wait_recv()
        here = place(y_pt, pieces[d])
        if d >= 2:
            forward_x.append(send(here, here, x_out.at[2 + d], x_in.at[2 + d], x_pt, md))
        over_core.append(send(here, here, core_out.at[8 + d], core_in.at[8 + d], core_pt, md))
        make(MARKS[4 + d], MARKS[5 + d])
    for d in range(4):
        (forward_y[d] if d < 2 else forward_x[d - 2]).wait_recv()
        here = place(xy_pt, pieces[d])
        over_core.append(send(here, here, core_out.at[12 + d], core_in.at[12 + d], core_pt, md))
    make(MARKS[8], phase_ref.shape[0])
    keep(phase_ref.shape[0] - 2).wait()
    keep(phase_ref.shape[0] - 1).wait()
    for copy in over_core:
        copy.wait_recv()
    for copy in sums + others + ups + over_x + over_y + over_core + forward_x + forward_y:
        copy.wait_send()


def exchange(scale, part, info, waves):
    rows, width = part.shape
    modes = waves.shape[0]
    sems = [n for n in (3, 3, 6, 6, 16, 7) for _ in range(2)]
    return pl.pallas_call(
        functools.partial(exchange_kernel, scale),
        out_shape=(
            jax.ShapeDtypeStruct((8 * rows, width), jnp.bfloat16),
            jax.ShapeDtypeStruct((8,) + info.shape, info.dtype),
            jax.ShapeDtypeStruct((8 * rows // TILE, modes, 2 * TILE), jnp.bfloat16),
        ),
        in_specs=[pl.BlockSpec(memory_space=pltpu.VMEM)] * 3,
        out_specs=(pl.BlockSpec(memory_space=pltpu.VMEM),) * 2 + (pl.BlockSpec(memory_space=pl.ANY),),
        scratch_shapes=[
            pltpu.VMEM((3, rows // 4, width), jnp.bfloat16),
            pltpu.VMEM((DEPTH, 8 * rows), jnp.float32),
            pltpu.VMEM((modes // TILE, TILE, TILE), jnp.float32),
            pltpu.VMEM((2, modes, 2 * TILE), jnp.bfloat16),
            pltpu.SemaphoreType.DMA((2,)),
        ]
        + [pltpu.SemaphoreType.DMA((n,)) for n in sems],
        compiler_params=pltpu.CompilerParams(
            collective_id=0, has_side_effects=True, vmem_limit_bytes=32 * 2**20
        ),
    )(part, info, waves)


def per_device(grid_index, wavenumbers, test_block, slab_counts):
    capacity = grid_index.shape[1]
    n_pt, n_md = lax.axis_size("pt"), lax.axis_size("md")
    y_scale = 1.0 / (32.0 * math.sqrt(M))
    w_scale = 1.0 / math.sqrt(capacity * n_pt)
    points = padded(grid_index, 1.0)
    waves = padded(wavenumbers, 1.0 / PERIOD)
    own = wavenumbers.shape[1] // n_pt
    mine = lax.dynamic_slice_in_dim(waves, lax.axis_index("pt") * own, own, 1)
    if (n_pt, n_md) == (8, 4):
        part = sketch_part(slab_counts, points.T, waves, test_block, jnp.bfloat16)
        info = jnp.concatenate(
            [grid_index, jnp.broadcast_to(slab_counts[:, None], (5, capacity))], axis=0
        )
        sketch, gathered, phase = exchange(y_scale, part, info, mine.T)
        per_slab = (gathered[:, 3, 0] + TILE - 1) // TILE
        ends = jnp.sum(jnp.where(jnp.arange(8)[:, None] <= jnp.arange(8)[None, :], per_slab[:, None], 0), axis=0)
        nth = jnp.minimum(jnp.arange(phase.shape[0], dtype=jnp.int32), ends[7] - 1)
        past = (ends[None, :] <= nth[:, None]).astype(jnp.int32)
        slab = jnp.sum(past, axis=1)
        order = slab * (capacity // TILE) + nth - jnp.sum(past * per_slab[None, :], axis=1)
        return product(w_scale, ends[7:], order.astype(jnp.int32), phase, sketch)
    else:
        counts = lax.all_gather(slab_counts, "pt", tiled=True)
        all_points = lax.all_gather(grid_index, "pt", axis=1, tiled=True)
        part = sketch_part(slab_counts, points.T, waves, test_block, jnp.float32)
        share = lax.psum_scatter(part, "md", scatter_dimension=0, tiled=True)
        share = (share * y_scale).astype(jnp.bfloat16)
        sketch = lax.all_gather(share, ("pt", "md"), tiled=True)
    return adjoint_part(w_scale, counts, mine.T, padded(all_points, 1.0), sketch, capacity)


def solution(mesh):
    placed = (P(None, "pt"), P(None, "md"), P("md", None), P("pt"))
    return jax.shard_map(
        per_device, mesh=mesh, in_specs=placed, out_specs=P(("md", "pt"), None), check_vma=False
    )
```
